32 devices in a mesh: ctx: 8 (over y, x, core), dp: 4 (over z).
Axes of the slice: x: 2, y: 2, z: 4, core: 2. Of those that a mesh axis runs over, the one named last changes fastest.
Arguments:
- hidden_in: bfloat16 [4, 2048, 2048], P('dp', 'ctx'), may hold values from -6 to 6
- queries: bfloat16 [4, 2048, 2048], P('dp', 'ctx'), may hold values from -1000 to 1000
- norm_gain: bfloat16 [2048], replicated, may hold values from 0.099609375 to 1.8984375
- weight_store: bfloat16 [4, 2048, 512], P('dp', 'ctx'), may hold values from -0.125 to 0.125
- owners: int32 [2], replicated, may hold values from 0 to 3, as said below
- doc_lengths: int32 [4, 4], P('dp'), may hold values from 1 to 1024, 2048 in all within a row
Outputs:
- attended: bfloat16 [4, 2048, 2048], P('dp', 'ctx')
The draws below stay inside these ranges and needn't reach their ends.
Inputs may be any that keep to these rules, and one draw needn't show every extreme that they name: `owners`: two different data ranks, one of them the last rank 4 - 1; the first owns the key projection, the second the value projection.
All inputs are finite; a program needn't handle non-finite values.
Results may differ from the reference program's by a relative error of at most 0.012.
Values may be sent and summed in bfloat16 or wider, within the bound.
No kernel may reach another device: no remote copies, remote signals or barrier semaphores. Data moves between devices by JAX's collectives and lax.ppermute only.
A program may use at most 64 MiB of HBM per device.

```python
import math
import jax
import jax.numpy as jnp
import numpy as np
from jax import lax

D = 2048
HQ = 16
HS = 128
REACH = 4
TOK_DEV = 256
KVW = 512
LENGTH = 2048
SPAN = 1024
NDOC = 4
SEQS = 4
N_CTX = 8
N_DP = 4


def draw_owners(key, part):
    other = jax.random.randint(jax.random.fold_in(key, 11), (), 0, N_DP - 1).astype(jnp.int32)
    flip = jax.random.randint(jax.random.fold_in(key, 12), (), 0, 2).astype(jnp.int32)
    last = jnp.int32(N_DP - 1)
    first_owner = jnp.where(flip == 0, other, last)
    second_owner = jnp.where(flip == 0, last, other)
    return jnp.stack([first_owner, second_owner]).astype(jnp.int32)


def draw_queries(key, part):
    shape_all = (N_DP, LENGTH, HQ * HS)
    values = jnp.clip(jax.random.normal(jax.random.fold_in(key, 4), shape_all, jnp.float32), -6.0, 6.0)
    return values.astype(jnp.bfloat16)


def levels(key, shape, cuts, least, largest):
    factor_of, own = 1.0, jax.random.fold_in(key, 6)
    for axis_at, shards_of in cuts:
        heights = jnp.exp(jax.random.uniform(jax.random.fold_in(own, axis_at), (shards_of,), jnp.float32, least / len(cuts), largest / len(cuts)))
        factor_of = factor_of * jnp.repeat(heights, shape[axis_at] // shards_of).reshape([-1 if axis == axis_at else 1 for axis in range(len(shape))])
    return factor_of


def profile(amount, total, bound, lean):
    portions = [(1 << 20) // math.isqrt(rank ** lean) + 1 for rank in range(2, amount + 1)]
    surplus, counts = total - bound - (amount - 1), [1] * (amount - 1)
    while surplus > 0:
        movable = [i for i in range(amount - 1) if counts[i] < bound]
        pool, budget = sum([portions[i] for i in movable]), surplus
        for i in movable:
            more = min(bound - counts[i], max(1, budget * portions[i] // pool), surplus)
            counts[i] = counts[i] + more
            surplus = surplus - more
    return np.array([bound] + counts)


def ragged(own_key, amount, total, most, slope):
    if amount == 2:
        one = jax.random.randint(own_key, (), max(1, total - most), min(most, total - 1) + 1)
        return jnp.stack([one, total - one])
    sizes = jnp.asarray(profile(amount, total, most, slope), jnp.int32)
    twos = (amount - 1) // 2
    giver, taker = sizes[1:1 + 2 * twos:2], sizes[2:2 + 2 * twos:2]
    slack = jnp.minimum(giver - 1, most - taker)
    moved = jax.random.randint(jax.random.fold_in(own_key, 1), (twos,), 0, 1 << 20) % (slack + 1)
    sizes = sizes.at[1:1 + 2 * twos:2].set(giver - moved).at[2:2 + 2 * twos:2].set(taker + moved)
    return sizes[jax.random.permutation(jax.random.fold_in(own_key, 2), amount)]


def scatter_about(key, shape, width, reach, split=(), kind=jnp.bfloat16):
    entries = jax.random.normal(key, shape, jnp.float32) * width
    if len(split) > 0:
        entries = levels(key, shape, split, -0.22, 0.18) * entries
    return jnp.clip(entries, min=-reach, max=reach).astype(kind)


def setup_inputs(seed: int = 0) -> dict:
    arg_keys = jax.random.split(jax.random.key(seed), 7)
    return {
        "hidden_in": scatter_about(arg_keys[0], (SEQS, LENGTH, D), 1.0, 6.0, ((0, 4), (1, 8))),
        "queries": draw_queries(jax.random.fold_in(arg_keys[6], 71), 0),
        "norm_gain": jnp.clip(1.0 + 0.18 * jax.random.normal(arg_keys[2], (D,), jnp.float32), 0.099609375, 1.8984375).astype(jnp.bfloat16),
        "weight_store": scatter_about(arg_keys[3], (N_DP, D, KVW), D ** -0.5, 0.125, ((0, 4), (1, 8))),
        "owners": draw_owners(jax.random.fold_in(arg_keys[6], 71), 0),
        "doc_lengths": jax.vmap(lambda own: ragged(own, NDOC, LENGTH, SPAN, 2))(jax.random.split(arg_keys[5], SEQS)).reshape((SEQS, NDOC)).astype(jnp.int32),
    }


def find_starts(lengths, positions):
    ends = jnp.cumsum(lengths)
    starts = (ends - lengths).astype(jnp.int32)
    below = starts[None, :] <= positions[:, None]
    return lax.optimization_barrier(jnp.max(jnp.where(below, starts[None, :], 0), axis=1)).astype(jnp.int32)

def attend_block(q_blk, k_blk, v_blk, allowed):
    tok_rows = q_blk.shape[0]
    kv_heads = k_blk.shape[1] // HS
    group = q_blk.shape[1] // (kv_heads * HS)
    q_four = q_blk.astype(jnp.float32).reshape(tok_rows, kv_heads, group, HS)
    k_three = k_blk.astype(jnp.float32).reshape(-1, kv_heads, HS)
    v_three = v_blk.astype(jnp.float32).reshape(-1, kv_heads, HS)
    score = jnp.einsum('tkgd,wkd->kgtw', q_four, k_three) * (1.0 / jnp.sqrt(jnp.float32(HS)))
    score = jnp.where(allowed[None, None], score, jnp.float32(-1e+30))
    top = lax.optimization_barrier(jnp.max(score, axis=-1, keepdims=True))
    weight = jnp.exp(score - top)
    total = lax.optimization_barrier(jnp.sum(weight, axis=-1))
    weight_b = weight.astype(jnp.bfloat16)
    summed = jnp.einsum('kgtw,wkd->kgtd', weight_b.astype(jnp.float32), v_three)
    result = (summed / total[..., None]).astype(jnp.bfloat16)
    return jnp.transpose(result, (2, 0, 1, 3)).reshape(tok_rows, -1)

def reference(hidden_in, queries, norm_gain, weight_store, owners, doc_lengths):
    key_weight = weight_store[owners[0]]
    value_weight = weight_store[owners[1]]
    gain = norm_gain.astype(jnp.float32)

    def one_sequence(args):
        tokens, query_rows, lengths = args
        xf = tokens.astype(jnp.float32)
        scaled = (xf * lax.rsqrt(lax.optimization_barrier(jnp.mean(xf * xf, axis=-1, keepdims=True)) + 1e-05) * gain).astype(jnp.bfloat16)
        keys = jnp.dot(scaled, key_weight, preferred_element_type=jnp.float32).astype(jnp.bfloat16)
        values = jnp.dot(scaled, value_weight, preferred_element_type=jnp.float32).astype(jnp.bfloat16)
        padding = jnp.zeros((REACH * TOK_DEV, keys.shape[1]), jnp.bfloat16)
        keys_pad = jnp.concatenate([padding, keys], axis=0)
        values_pad = jnp.concatenate([padding, values], axis=0)
        positions = jnp.arange(LENGTH, dtype=jnp.int32)
        starts = find_starts(lengths, positions)

        def one_block(block):
            first = (block * TOK_DEV).astype(jnp.int32)
            q_blk = lax.dynamic_slice_in_dim(query_rows, first, TOK_DEV, 0)
            k_blk = lax.dynamic_slice_in_dim(keys_pad, first, (REACH + 1) * TOK_DEV, 0)
            v_blk = lax.dynamic_slice_in_dim(values_pad, first, (REACH + 1) * TOK_DEV, 0)
            q_pos = first + jnp.arange(TOK_DEV, dtype=jnp.int32)
            k_pos = first - REACH * TOK_DEV + jnp.arange((REACH + 1) * TOK_DEV, dtype=jnp.int32)
            q_start = lax.dynamic_slice_in_dim(starts, first, TOK_DEV, 0)
            allowed = (k_pos[None, :] >= q_start[:, None]) & (k_pos[None, :] <= q_pos[:, None])
            return attend_block(q_blk, k_blk, v_blk, allowed)
        blocks = lax.map(one_block, jnp.arange(N_CTX, dtype=jnp.int32))
        return blocks.reshape(LENGTH, -1)
    return lax.map(one_sequence, (hidden_in, queries, doc_lengths))
```

```python
import functools

import jax
import jax.numpy as jnp
import numpy as np
from jax import lax
from jax.experimental import pallas as pl
from jax.experimental.pallas import tpu as pltpu
from jax.sharding import Mesh
from jax.sharding import PartitionSpec as P

HS = 128
REACH = 4
CORES = 2
SWAP = [(0, 1), (1, 0)]
MASKED = -1e30


def attend_kernel(back, chip_ref, docs_ref, q_ref, *refs):
    kv_refs = refs[: back + 1]
    out_ref, bias_ref = refs[back + 1], refs[back + 2]
    tokens = q_ref.shape[0]
    block = tokens // CORES
    half = kv_refs[0].shape[1] // 2
    heads = half // HS
    group = q_ref.shape[1] // half
    width = (REACH + 1) * block
    factor = 1.4426950408889634 / np.sqrt(HS)
    first_key = (chip_ref[0] - back) * tokens
    for b in range(CORES):
        q_pos = back * tokens + b * block + lax.broadcasted_iota(jnp.int32, (block, 1), 0)
        start = jnp.full((block, 1), -(2**30), jnp.int32)
        prefix = -first_key
        for d in range(docs_ref.shape[0]):
            start = jnp.where(q_pos >= prefix, prefix, start)
            prefix = prefix + docs_ref[d]
        k_pos = b * block + lax.broadcasted_iota(jnp.int32, (block, width), 1)
        allowed = (k_pos >= start) & (k_pos <= q_pos)
        bias_ref[b] = jnp.where(allowed, 0.0, MASKED)

    def window(low, columns):
        parts = []
        for i, ref in enumerate(kv_refs):
            lo, hi = max(low - i * tokens, 0), min(low + width - i * tokens, tokens)
            if lo < hi:
                parts.append(ref[lo:hi, columns])
        return jnp.concatenate(parts, axis=0)

    for h in range(heads):
        for b in range(CORES):
            keys = window(b * block, pl.ds(h * HS, HS))
            values = window(b * block, pl.ds(half + h * HS, HS))
            for g in range(group):
                at = pl.ds((h * group + g) * HS, HS)
                rows = pl.ds(b * block, block)
                score = lax.dot_general(
                    q_ref[rows, at], keys, (((1,), (1,)), ((), ())), preferred_element_type=jnp.float32
                )
                score = score + bias_ref[b]
                top = jnp.max(score, axis=-1, keepdims=True)
                weight = jnp.exp2((score - top) * factor)
                total = jnp.sum(weight, axis=-1, keepdims=True)
                summed = jnp.dot(weight.astype(jnp.bfloat16), values, preferred_element_type=jnp.float32)
                out_ref[rows, at] = (summed / total).astype(jnp.bfloat16)


def attend(chip, docs, q, kvs):
    tokens, block = q.shape[0], q.shape[0] // CORES
    smem = pl.BlockSpec(memory_space=pltpu.SMEM)
    vmem = pl.BlockSpec(memory_space=pltpu.VMEM)
    return pl.pallas_call(
        functools.partial(attend_kernel, len(kvs) - 1),
        out_shape=jax.ShapeDtypeStruct(q.shape, jnp.bfloat16),
        in_specs=[smem, smem, vmem] + [vmem] * len(kvs),
        out_specs=vmem,
        scratch_shapes=[pltpu.VMEM((CORES, block, (REACH + 1) * block), jnp.float32)],
        compiler_params=pltpu.CompilerParams(vmem_limit_bytes=48 << 20),
        name="attend",
    )(chip, docs, q, *kvs)


def both_cores(core, own, other, axis):
    return jnp.where(
        core == 0, jnp.concatenate([own, other], axis), jnp.concatenate([other, own], axis)
    )


def local(n_chip, n_dp, hidden_in, queries, norm_gain, weight_store, owners, doc_lengths):
    core = lax.axis_index("core")
    chip = lax.axis_index("chip")
    rank = lax.axis_index("dp")
    slot = weight_store[0]
    half = slot.shape[1] // CORES
    slot_own = lax.dynamic_slice_in_dim(slot, core * half, half, 1)
    slot_other = lax.dynamic_slice_in_dim(slot, (1 - core) * half, half, 1)
    chunk = both_cores(core, slot_own, lax.ppermute(slot_other, "core", SWAP), 0)
    slots = [chunk] + [
        lax.ppermute(chunk, "dp", [(i, (i + k) % n_dp) for i in range(n_dp)]) for k in range(1, n_dp)
    ]

    xf = hidden_in[0].astype(jnp.float32)
    scaled = (
        xf
        * lax.rsqrt(jnp.mean(xf * xf, axis=-1, keepdims=True) + 1e-05)
        * norm_gain.astype(jnp.float32)
    ).astype(jnp.bfloat16)
    scaled = both_cores(core, scaled, lax.ppermute(scaled, "core", SWAP), 0)
    q_half = queries.shape[2] // CORES
    q_own = lax.dynamic_slice_in_dim(queries[0], core * q_half, q_half, 1)
    q_other = lax.dynamic_slice_in_dim(queries[0], (1 - core) * q_half, q_half, 1)
    q = both_cores(core, q_own, lax.ppermute(q_other, "core", SWAP), 0)

    def owned(owner):
        at = lax.rem(rank - owner + n_dp, n_dp)
        chosen = slots[0]
        for k in range(1, n_dp):
            chosen = jnp.where(at == k, slots[k], chosen)
        return chosen

    weights = jnp.concatenate([owned(owners[0]), owned(owners[1])], axis=1)
    rows = weights.shape[0]
    total = jnp.zeros((scaled.shape[0], weights.shape[1]), jnp.float32)
    for k in range(n_chip):
        part = weights
        if k:
            part = lax.ppermute(weights, "chip", [(i, i ^ k) for i in range(n_chip)])
        columns = lax.dynamic_slice_in_dim(scaled, (chip ^ k) * rows, rows, 1)
        total = total + jnp.dot(columns, part, preferred_element_type=jnp.float32)
    kv = total.astype(jnp.bfloat16)
    back = REACH // CORES
    kvs = [
        lax.ppermute(kv, "chip", [(i, i + by) for i in range(n_chip - by)]) for by in range(back, 0, -1)
    ] + [kv]
    out = attend(chip[None], doc_lengths[0], q, kvs)
    tok = hidden_in.shape[1]
    mine = lax.dynamic_slice_in_dim(out, core * tok, tok, 0)
    theirs = lax.dynamic_slice_in_dim(out, (1 - core) * tok, tok, 0)
    return both_cores(core, mine, lax.ppermute(theirs, "core", SWAP), 1)[None]


def solution(mesh):
    n_ctx, n_dp = mesh.shape["ctx"], mesh.shape["dp"]
    n_chip = n_ctx // CORES
    view = Mesh(mesh.devices.reshape(n_chip, CORES, n_dp), ("chip", "core", "dp"))
    rows = P("dp", ("chip", "core"), None)
    return jax.shard_map(
        functools.partial(local, n_chip, n_dp),
        mesh=view,
        in_specs=(rows, rows, P(), rows, P(), P("dp", None)),
        out_specs=rows,
        check_vma=False,
    )
```

```python
import functools

import jax
import jax.numpy as jnp
import numpy as np
from jax import lax
from jax.experimental import pallas as pl
from jax.experimental.pallas import tpu as pltpu
from jax.sharding import PartitionSpec as P

HS = 128
REACH = 4
CORES = 2
MASKED = -1e30
SMEM = pl.BlockSpec(memory_space=pltpu.SMEM)
VMEM = pl.BlockSpec(memory_space=pltpu.VMEM)


def cost(flops):
    return pl.CostEstimate(flops=int(flops), bytes_accessed=1 << 20, transcendentals=0)


def attend_kernel(head, at_ref, docs_ref, own_ref, other_ref, *refs):
    kv_refs, out_ref, bias_ref = refs[:-2], refs[-2], refs[-1]
    core = lax.rem(at_ref[0], CORES)
    block = own_ref.shape[0]
    tokens = kv_refs[0].shape[0]
    back = len(kv_refs) - 1
    group = out_ref.shape[2] // HS
    width = (REACH + 1) * block
    factor = 1.4426950408889634 / np.sqrt(HS)
    first_key = (at_ref[0] // CORES - back) * tokens
    for b in range(CORES):
        q_pos = back * tokens + b * block + lax.broadcasted_iota(jnp.int32, (block, 1), 0)
        start = jnp.full((block, 1), -(2**30), jnp.int32)
        prefix = -first_key
        for d in range(docs_ref.shape[0]):
            start = jnp.where(q_pos >= prefix, prefix, start)
            prefix = prefix + docs_ref[d]
        k_pos = b * block + lax.broadcasted_iota(jnp.int32, (block, width), 1)
        bias_ref[b] = jnp.where((k_pos >= start) & (k_pos <= q_pos), 0.0, MASKED)

    def window(low, columns):
        parts = []
        for i, ref in enumerate(kv_refs):
            lo, hi = max(low - i * tokens, 0), min(low + width - i * tokens, tokens)
            if lo < hi:
                parts.append(ref[lo:hi, columns])
        return jnp.concatenate(parts, axis=0)

    for b in range(CORES):
        keys = window(b * block, pl.ds(0, HS))
        values = window(b * block, pl.ds(HS, HS))
        for g in range(group):
            own = own_ref[:, pl.ds(pl.multiple_of(((head * CORES + core) * group + g) * HS, HS), HS)]
            column = (head * group + g) * HS
            query = jnp.where(core == b, own, other_ref[:, column : column + HS])
            score = lax.dot_general(query, keys, (((1,), (1,)), ((), ())), preferred_element_type=jnp.float32)
            score = score + bias_ref[b]
            top = jnp.max(score, axis=-1, keepdims=True)
            weight = jnp.exp2((score - top) * factor)
            total = jnp.sum(weight, axis=-1, keepdims=True)
            summed = jnp.dot(weight.astype(jnp.bfloat16), values, preferred_element_type=jnp.float32)
            out_ref[core ^ b, :, g * HS : (g + 1) * HS] = (summed / total).astype(jnp.bfloat16)


def attend(head, heads, at, docs, own, other, kvs):
    block = own.shape[0]
    return pl.pallas_call(
        functools.partial(attend_kernel, head),
        out_shape=jax.ShapeDtypeStruct((CORES, own.shape[0], other.shape[1] // heads), jnp.bfloat16),
        in_specs=[SMEM] * 2 + [VMEM] * (2 + len(kvs)),
        out_specs=VMEM,
        scratch_shapes=[pltpu.VMEM((CORES, block, (REACH + 1) * block), jnp.float32)],
        compiler_params=pltpu.CompilerParams(vmem_limit_bytes=32 << 20),
        cost_estimate=cost(5e9),
        name="attend",
    )(at, docs, own, other, *kvs)


def both_cores(core, own, other, axis):
    return jnp.where(
        core == 0, jnp.concatenate([own, other], axis), jnp.concatenate([other, own], axis)
    )


def exchange(x, bit, size, name):
    with jax.named_scope(name):
        return lax.ppermute(x, "ctx", [(i, i ^ bit) for i in range(size)])


def after(x, *others):
    return lax.optimization_barrier((x, others))[0]


def local(n_ctx, n_dp, hidden_in, queries, norm_gain, weight_store, owners, doc_lengths):
    at = lax.axis_index("ctx")
    core = at % CORES
    rank = lax.axis_index("dp")
    slot = weight_store[0]
    rows = slot.shape[0]
    heads = slot.shape[1] // (CORES * HS)
    chips = n_ctx // CORES
    back = REACH // CORES

    pieces = [slot[:, h * CORES * HS : (h + 1) * CORES * HS] for h in range(heads)]

    def over_dp(h, piece):
        slots = [piece]
        for k in range(1, n_dp):
            with jax.named_scope(f"z{h}_{k}"):
                slots.append(lax.ppermute(piece, "dp", [(i, i ^ k) for i in range(n_dp)]))
        return slots

    def owned(slots, owner):
        chosen = slots[0]
        for k in range(1, n_dp):
            chosen = jnp.where((rank ^ owner) == k, slots[k], chosen)
        return chosen

    def forward(x, by, name):
        with jax.named_scope(name):
            return lax.ppermute(x, "ctx", [(i, i + by * CORES) for i in range(n_ctx - by * CORES)])

    slots = over_dp(0, pieces[0])
    xf = hidden_in[0].astype(jnp.float32)
    scaled = (
        xf
        * lax.rsqrt(jnp.mean(xf * xf, axis=-1, keepdims=True) + 1e-05)
        * norm_gain.astype(jnp.float32)
    ).astype(jnp.bfloat16)
    scaled = both_cores(core, scaled, exchange(scaled, 1, n_ctx, "s"), 0)
    columns = [
        jnp.concatenate(
            [lax.dynamic_slice_in_dim(scaled, (at ^ (o * CORES) ^ c) * rows, rows, 1) for c in range(CORES)], axis=1
        )
        for o in range(chips)
    ]
    share = queries.shape[2] // (heads * CORES)
    q_other = jnp.concatenate(
        [lax.dynamic_slice_in_dim(queries[0], (h * CORES + 1 - core) * share, share, 1) for h in range(heads)], axis=1
    )
    q_other = exchange(q_other, 1, n_ctx, "q")

    bits = [CORES << i for i in reversed(range(chips.bit_length() - 1))]
    window = []
    for h in range(heads):
        key, value = owned(slots, owners[0]), owned(slots, owners[1])
        low = jnp.concatenate([key[:, :HS], value[:, :HS]], axis=1)
        high = jnp.concatenate([key[:, HS:], value[:, HS:]], axis=1)
        mine, theirs = jnp.where(core == 0, low, high), jnp.where(core == 0, high, low)
        if h + 1 < heads:
            piece, theirs = lax.optimization_barrier((pieces[h + 1], theirs))
            slots = over_dp(h + 1, piece)
        parts, order = [jnp.concatenate([mine, exchange(theirs, 1, n_ctx, f"c{h}")], axis=0)], [0]
        if h == 0:
            for o in range(CORES, n_ctx, CORES):
                parts.append(exchange(parts[0], o, n_ctx, f"w{h}_{o}"))
                order.append(o)
            slots, columns = lax.optimization_barrier((slots, columns))
        else:
            for bit in bits:
                for i, (o, p) in enumerate(zip(list(order), list(parts))):
                    if i:
                        p = after(p, parts[-1])
                    parts.append(exchange(p, bit, n_ctx, f"w{h}_{bit}_{i}"))
                    order.append(o ^ bit)
        total = None
        for o, part in zip(order, parts):
            product = jnp.dot(columns[o // CORES], part, preferred_element_type=jnp.float32)
            total = product if total is None else total + product
        kv = total.astype(jnp.bfloat16)
        window.append([forward(kv, by, f"kv{h}_{by}") for by in range(back, 0, -1)] + [kv])
    outs = []
    for h in range(heads):
        own = queries[0]
        if h + 1 < heads:
            own = after(own, window[h + 1][-1])
        out = attend(h, heads, at[None], doc_lengths[0], own, q_other, window[h])
        outs.append(both_cores(core, out[0], exchange(out[1], 1, n_ctx, f"o{h}"), 1))
    return jnp.concatenate(outs, axis=1)[None]


def solution(mesh):
    rows = P("dp", "ctx", None)
    return jax.shard_map(
        functools.partial(local, mesh.shape["ctx"], mesh.shape["dp"]),
        mesh=mesh,
        in_specs=(rows, rows, P(), rows, P(), P("dp", None)),
        out_specs=rows,
        check_vma=False,
    )
```

```python
import functools

import jax
import jax.numpy as jnp
import numpy as np
from jax import lax
from jax.experimental import pallas as pl
from jax.experimental.pallas import tpu as pltpu
from jax.sharding import PartitionSpec as P

HS = 128
REACH = 4
CORES = 2
MASKED = -1e30
SMEM = pl.BlockSpec(memory_space=pltpu.SMEM)
VMEM = pl.BlockSpec(memory_space=pltpu.VMEM)


def cost(flops):
    return pl.CostEstimate(flops=int(flops), bytes_accessed=1 << 20, transcendentals=0)


def attend_kernel(head, at_ref, docs_ref, own_ref, other_ref, *refs):
    kv_refs, out_ref, bias_ref = refs[:-2], refs[-2], refs[-1]
    core = lax.rem(at_ref[0], CORES)
    block = own_ref.shape[0]
    tokens = kv_refs[0].shape[0]
    back = len(kv_refs) - 1
    group = out_ref.shape[2] // HS
    width = (REACH + 1) * block
    factor = 1.4426950408889634 / np.sqrt(HS)
    first_key = (at_ref[0] // CORES - back) * tokens
    for b in range(CORES):
        q_pos = back * tokens + b * block + lax.broadcasted_iota(jnp.int32, (block, 1), 0)
        start = jnp.full((block, 1), -(2**30), jnp.int32)
        prefix = -first_key
        for d in range(docs_ref.shape[0]):
            start = jnp.where(q_pos >= prefix, prefix, start)
            prefix = prefix + docs_ref[d]
        k_pos = b * block + lax.broadcasted_iota(jnp.int32, (block, width), 1)
        bias_ref[b] = jnp.where((k_pos >= start) & (k_pos <= q_pos), 0.0, MASKED)

    def window(low, columns):
        parts = []
        for i, ref in enumerate(kv_refs):
            lo, hi = max(low - i * tokens, 0), min(low + width - i * tokens, tokens)
            if lo < hi:
                parts.append(ref[lo:hi, columns])
        return jnp.concatenate(parts, axis=0)

    for b in range(CORES):
        keys = window(b * block, pl.ds(0, HS))
        values = window(b * block, pl.ds(HS, HS))
        values = jnp.concatenate([values, jnp.ones_like(values)], axis=1)
        for g in range(group):
            own = own_ref[:, pl.ds(pl.multiple_of(((head * CORES + core) * group + g) * HS, HS), HS)]
            column = (head * group + g) * HS
            query = jnp.where(core == b, own, other_ref[:, column : column + HS])
            score = lax.dot_general(query, keys, (((1,), (1,)), ((), ())), preferred_element_type=jnp.float32)
            score = score + bias_ref[b]
            top = jnp.max(score, axis=-1, keepdims=True)
            weight = jnp.exp2((score - top) * factor)
            summed = jnp.dot(weight.astype(jnp.bfloat16), values, preferred_element_type=jnp.float32)
            out_ref[core ^ b, :, g * HS : (g + 1) * HS] = (summed[:, :HS] / summed[:, HS:]).astype(jnp.bfloat16)


def attend(head, heads, at, docs, own, other, kvs):
    block = own.shape[0]
    return pl.pallas_call(
        functools.partial(attend_kernel, head),
        out_shape=jax.ShapeDtypeStruct((CORES, own.shape[0], other.shape[1] // heads), jnp.bfloat16),
        in_specs=[SMEM] * 2 + [VMEM] * (2 + len(kvs)),
        out_specs=VMEM,
        scratch_shapes=[pltpu.VMEM((CORES, block, (REACH + 1) * block), jnp.float32)],
        compiler_params=pltpu.CompilerParams(vmem_limit_bytes=32 << 20),
        cost_estimate=cost(5e9),
        name="attend",
    )(at, docs, own, other, *kvs)


def both_cores(core, own, other, axis):
    return jnp.where(
        core == 0, jnp.concatenate([own, other], axis), jnp.concatenate([other, own], axis)
    )


def exchange(x, bit, size, name):
    with jax.named_scope(name):
        return lax.ppermute(x, "ctx", [(i, i ^ bit) for i in range(size)])


def after(x, *others):
    return lax.optimization_barrier((x, others))[0]


def local(n_ctx, n_dp, hidden_in, queries, norm_gain, weight_store, owners, doc_lengths):
    at = lax.axis_index("ctx")
    core = at % CORES
    rank = lax.axis_index("dp")
    slot = weight_store[0]
    rows = slot.shape[0]
    heads = slot.shape[1] // (CORES * HS)
    chips = n_ctx // CORES
    back = REACH // CORES

    pieces = [slot[:, : CORES * HS]]

    def over_dp(h, piece):
        slots = [piece]
        for k in range(1, n_dp):
            with jax.named_scope(f"z{h}_{k}"):
                slots.append(lax.ppermute(piece, "dp", [(i, i ^ k) for i in range(n_dp)]))
        return slots

    def owned(slots, owner):
        chosen = slots[0]
        for k in range(1, n_dp):
            chosen = jnp.where((rank ^ owner) == k, slots[k], chosen)
        return chosen

    def forward(x, by, name):
        with jax.named_scope(name):
            return lax.ppermute(x, "ctx", [(i, i + by * CORES) for i in range(n_ctx - by * CORES)])

    slots = over_dp(0, pieces[0])
    xf = hidden_in[0].astype(jnp.float32)
    scaled = (
        xf
        * lax.rsqrt(jnp.mean(xf * xf, axis=-1, keepdims=True) + 1e-05)
        * norm_gain.astype(jnp.float32)
    ).astype(jnp.bfloat16)
    slots, scaled = lax.optimization_barrier((slots, scaled))
    slot = after(slot, scaled)
    pieces += [slot[:, h * CORES * HS : (h + 1) * CORES * HS] for h in range(1, heads)]
    scaled_other = exchange(scaled, 1, n_ctx, "s")
    share = queries.shape[2] // (heads * CORES)

    bits = [CORES << i for i in reversed(range(chips.bit_length() - 1))]
    window = []
    for h in range(heads):
        key, value = owned(slots, owners[0]), owned(slots, owners[1])
        low = jnp.concatenate([key[:, :HS], value[:, :HS]], axis=1)
        high = jnp.concatenate([key[:, HS:], value[:, HS:]], axis=1)
        mine, theirs = jnp.where(core == 0, low, high), jnp.where(core == 0, high, low)
        if h + 1 < heads:
            piece, theirs = lax.optimization_barrier((pieces[h + 1], theirs))
            slots = over_dp(h + 1, piece)
        if h:
            q_all = after(queries[0], theirs)
            q_other = jnp.concatenate(
                [lax.dynamic_slice_in_dim(q_all, (i * CORES + 1 - core) * share, share, 1) for i in range(heads)], axis=1
            )
            q_other = exchange(q_other, 1, n_ctx, "q")
        parts, order = [jnp.concatenate([mine, exchange(theirs, 1, n_ctx, f"c{h}")], axis=0)], [0]
        if h == 0:
            parts[0], scaled_other = lax.optimization_barrier((parts[0], scaled_other))
            both = both_cores(core, scaled, scaled_other, 0)
            columns = [
                jnp.concatenate(
                    [lax.dynamic_slice_in_dim(both, (at ^ (o * CORES) ^ c) * rows, rows, 1) for c in range(CORES)],
                    axis=1,
                )
                for o in range(chips)
            ]
            for o in range(CORES, n_ctx, CORES):
                parts.append(exchange(parts[0], o, n_ctx, f"w{h}_{o}"))
                order.append(o)
            slots, columns = lax.optimization_barrier((slots, columns))
            parts = list(lax.optimization_barrier(parts))
        else:
            for bit in bits:
                for i, (o, p) in enumerate(zip(list(order), list(parts))):
                    if i:
                        p = after(p, parts[-1])
                    parts.append(exchange(p, bit, n_ctx, f"w{h}_{bit}_{i}"))
                    order.append(o ^ bit)
        total = None
        for o, part in zip(order, parts):
            product = jnp.dot(columns[o // CORES], part, preferred_element_type=jnp.float32)
            total = product if total is None else total + product
        kv = total.astype(jnp.bfloat16)
        window.append([forward(kv, by, f"kv{h}_{by}") for by in range(back, 0, -1)] + [kv])
    outs = []
    for h in range(heads):
        own = queries[0]
        if h + 1 < heads:
            own = after(own, window[h + 1][-1])
        out = attend(h, heads, at[None], doc_lengths[0], own, q_other, window[h])
        outs.append(both_cores(core, out[0], exchange(out[1], 1, n_ctx, f"o{h}"), 1))
    return jnp.concatenate(outs, axis=1)[None]


def solution(mesh):
    rows = P("dp", "ctx", None)
    return jax.shard_map(
        functools.partial(local, mesh.shape["ctx"], mesh.shape["dp"]),
        mesh=mesh,
        in_specs=(rows, rows, P(), rows, P(), P("dp", None)),
        out_specs=rows,
        check_vma=False,
    )
```

```python
import functools

import jax
import jax.numpy as jnp
import numpy as np
from jax import lax
from jax.experimental import pallas as pl
from jax.experimental.pallas import tpu as pltpu
from jax.sharding import PartitionSpec as P

HS = 128
REACH = 4
CORES = 2
MASKED = -1e30
SMEM = pl.BlockSpec(memory_space=pltpu.SMEM)
VMEM = pl.BlockSpec(memory_space=pltpu.VMEM)


def cost(flops):
    return pl.CostEstimate(flops=int(flops), bytes_accessed=1 << 20, transcendentals=0)


def attend_kernel(head, turns, at_ref, docs_ref, own_ref, other_ref, *refs):
    kv_refs, out_refs, bias_ref = refs[: -len(turns) - 1], refs[-len(turns) - 1 : -1], refs[-1]
    core = lax.rem(at_ref[0], CORES)
    block = own_ref.shape[0]
    tokens = kv_refs[0].shape[0]
    back = len(kv_refs) - 1
    group = out_refs[0].shape[1] // HS
    width = (REACH + 1) * block
    factor = 1.4426950408889634 / np.sqrt(HS)
    first_key = (at_ref[0] // CORES - back) * tokens

    def window(low, columns):
        parts = []
        for i, ref in enumerate(kv_refs):
            lo, hi = max(low - i * tokens, 0), min(low + width - i * tokens, tokens)
            if lo < hi:
                parts.append(ref[lo:hi, columns])
        return jnp.concatenate(parts, axis=0)

    def attend_block(b, turn, out_ref):
        q_pos = back * tokens + b * block + lax.broadcasted_iota(jnp.int32, (block, 1), 0)
        start = jnp.full((block, 1), -(2**30), jnp.int32)
        prefix = -first_key
        for d in range(docs_ref.shape[0]):
            start = jnp.where(q_pos >= prefix, prefix, start)
            prefix = prefix + docs_ref[d]
        k_pos = b * block + lax.broadcasted_iota(jnp.int32, (block, width), 1)
        bias_ref[...] = jnp.where((k_pos >= start) & (k_pos <= q_pos), 0.0, MASKED)
        keys = window(b * block, pl.ds(0, HS))
        values = window(b * block, pl.ds(HS, HS))
        values = jnp.concatenate([values, jnp.ones_like(values)], axis=1)
        for g in range(group):
            query = (other_ref if turn else own_ref)[:, g * HS : (g + 1) * HS]
            score = lax.dot_general(query, keys, (((1,), (1,)), ((), ())), preferred_element_type=jnp.float32)
            score = score + bias_ref[...]
            top = jnp.max(score, axis=-1, keepdims=True)
            weight = jnp.exp2((score - top) * factor)
            summed = jnp.dot(weight.astype(jnp.bfloat16), values, preferred_element_type=jnp.float32)
            out_ref[:, g * HS : (g + 1) * HS] = (summed[:, :HS] / summed[:, HS:]).astype(jnp.bfloat16)

    for turn, out_ref in zip(turns, out_refs):
        for b in range(CORES):
            pl.when((core ^ turn) == b)(functools.partial(attend_block, b, turn, out_ref))


def attend(head, heads, turns, at, docs, own, other, kvs):
    block = own.shape[0]
    share = other.shape[1] // heads

    def whole(x):
        return pl.BlockSpec(x.shape, lambda i, at: (0,) * x.ndim)

    return pl.pallas_call(
        functools.partial(attend_kernel, head, turns),
        out_shape=[jax.ShapeDtypeStruct((block, share), jnp.bfloat16)] * len(turns),
        grid_spec=pltpu.PrefetchScalarGridSpec(
            num_scalar_prefetch=1,
            grid=(1,),
            in_specs=[
                SMEM,
                pl.BlockSpec((block, share), lambda i, at: (0, head * CORES + lax.rem(at[0], CORES))),
                pl.BlockSpec((block, share), lambda i, at: (0, head)),
            ]
            + [whole(x) for x in kvs],
            out_specs=[pl.BlockSpec((block, share), lambda i, at: (0, 0))] * len(turns),
            scratch_shapes=[pltpu.VMEM((block, (REACH + 1) * block), jnp.float32)],
        ),
        compiler_params=pltpu.CompilerParams(vmem_limit_bytes=32 << 20),
        cost_estimate=cost(2.5e9 * len(turns)),
        name="attend",
    )(at, docs, own, other, *kvs)


def both_cores(core, own, other, axis):
    return jnp.where(
        core == 0, jnp.concatenate([own, other], axis), jnp.concatenate([other, own], axis)
    )


def exchange(x, bit, size, name):
    with jax.named_scope(name):
        return lax.ppermute(x, "ctx", [(i, i ^ bit) for i in range(size)])


def after(x, *others):
    return lax.optimization_barrier((x, others))[0]


def local(n_ctx, n_dp, hidden_in, queries, norm_gain, weight_store, owners, doc_lengths):
    at = lax.axis_index("ctx")
    core = at % CORES
    rank = lax.axis_index("dp")
    slot = weight_store[0]
    rows = slot.shape[0]
    heads = slot.shape[1] // (CORES * HS)
    chips = n_ctx // CORES
    back = REACH // CORES

    pieces = [slot[:, : CORES * HS]]

    def over_dp(h, piece, steps):
        slots = []
        for k in steps:
            with jax.named_scope(f"z{h}_{k}"):
                slots.append(lax.ppermute(piece, "dp", [(i, i ^ k) for i in range(n_dp)]))
        return slots

    def owned(slots, owner):
        chosen = slots[0]
        for k in range(1, n_dp):
            chosen = jnp.where((rank ^ owner) == k, slots[k], chosen)
        return chosen

    def forward(x, by, name):
        with jax.named_scope(name):
            return lax.ppermute(x, "ctx", [(i, i + by * CORES) for i in range(n_ctx - by * CORES)])

    slots = [pieces[0]] + over_dp(0, pieces[0], range(1, n_dp))
    xf = hidden_in[0].astype(jnp.float32)
    scaled = (
        xf
        * lax.rsqrt(jnp.mean(xf * xf, axis=-1, keepdims=True) + 1e-05)
        * norm_gain.astype(jnp.float32)
    ).astype(jnp.bfloat16)
    slots, scaled = lax.optimization_barrier((slots, scaled))
    slot = after(slot, scaled)
    pieces += [slot[:, h * CORES * HS : (h + 1) * CORES * HS] for h in range(1, heads)]
    scaled_other = exchange(scaled, 1, n_ctx, "s")
    share = queries.shape[2] // (heads * CORES)

    bits = [CORES << i for i in reversed(range(chips.bit_length() - 1))]
    window = []
    for h in range(heads):
        key, value = owned(slots, owners[0]), owned(slots, owners[1])
        low = jnp.concatenate([key[:, :HS], value[:, :HS]], axis=1)
        high = jnp.concatenate([key[:, HS:], value[:, HS:]], axis=1)
        mine, theirs = jnp.where(core == 0, low, high), jnp.where(core == 0, high, low)
        if h + 1 < heads:
            piece, theirs = lax.optimization_barrier((pieces[h + 1], theirs))
            slots = [piece] + over_dp(h + 1, piece, range(1, n_dp - 1))
        if h:
            q_all = after(queries[0], theirs)
            q_other = jnp.concatenate(
                [lax.dynamic_slice_in_dim(q_all, (i * CORES + 1 - core) * share, share, 1) for i in range(heads)], axis=1
            )
            q_other = exchange(q_other, 1, n_ctx, "q")
        parts, order = [jnp.concatenate([mine, exchange(theirs, 1, n_ctx, f"c{h}")], axis=0)], [0]
        if h == 0:
            parts[0], scaled_other = lax.optimization_barrier((parts[0], scaled_other))
            both = both_cores(core, scaled, scaled_other, 0)
            columns = [
                jnp.concatenate(
                    [lax.dynamic_slice_in_dim(both, (at ^ (o * CORES) ^ c) * rows, rows, 1) for c in range(CORES)],
                    axis=1,
                )
                for o in range(chips)
            ]
            slots += over_dp(h + 1, after(piece, parts[0]), range(n_dp - 1, n_dp))
            for o in range(CORES, n_ctx, CORES):
                parts.append(exchange(parts[0], o, n_ctx, f"w{h}_{o}"))
                order.append(o)
            slots, columns = lax.optimization_barrier((slots, columns))
            parts = list(lax.optimization_barrier(parts))
        else:
            for bit in bits:
                for i, (o, p) in enumerate(zip(list(order), list(parts))):
                    if i:
                        p = after(p, parts[-1])
                    parts.append(exchange(p, bit, n_ctx, f"w{h}_{bit}_{i}"))
                    order.append(o ^ bit)
        total = None
        for o, part in zip(order, parts):
            product = jnp.dot(columns[o // CORES], part, preferred_element_type=jnp.float32)
            total = product if total is None else total + product
        kv = total.astype(jnp.bfloat16)
        window.append([forward(kv, by, f"kv{h}_{by}") for by in range(back, 0, -1)] + [kv])
    outs = []
    for h in range(heads):
        own = queries[0]
        if h + 1 < heads:
            own = after(own, window[h + 1][-1])
        rest = (at[None], doc_lengths[0], own, q_other, window[h])
        if h + 1 < heads:
            theirs, mine = attend(h, heads, (1, 0), *rest)
        else:
            (theirs,) = attend(h, heads, (1,), *rest)
            (mine,) = attend(h, heads, (0,), *rest[:3], after(q_other, theirs), rest[4])
        outs.append(both_cores(core, mine, exchange(theirs, 1, n_ctx, f"o{h}"), 1))
    return jnp.concatenate(outs, axis=1)[None]


def solution(mesh):
    rows = P("dp", "ctx", None)
    return jax.shard_map(
        functools.partial(local, mesh.shape["ctx"], mesh.shape["dp"]),
        mesh=mesh,
        in_specs=(rows, rows, P(), rows, P(), P("dp", None)),
        out_specs=rows,
        check_vma=False,
    )
```
